256 devices in a mesh: gx: 2 (over core), gy: 4 (over x), gz: 32 (over z, y).
Axes of the slice: x: 4, y: 4, z: 8, core: 2. Of those that a mesh axis runs over, the one named last changes fastest.
Arguments:
- a_blocks: bfloat16 [4, 8, 64, 64, 2048], P('gx', 'gy', 'gz'), may hold values from -0.15625 to 0.15625
- a_cols: int32 [4, 8, 64, 32], P('gx', 'gy', 'gz'), may hold values from 0 to 26, as said below
- a_count: int32 [4, 8, 64], P('gx', 'gy', 'gz'), may hold values from 14 to 27
- p_blocks: bfloat16 [4, 8, 64, 64, 512], P('gx', 'gy', 'gz'), may hold values from -0.75 to 0.75
- p_cols: int32 [4, 8, 64, 8], P('gx', 'gy', 'gz'), may hold values from 0 to 7, as said below
- p_count: int32 [4, 8, 64], P('gx', 'gy', 'gz'), may hold values from 1 to 8
- coarse_row: int32 [2, 4, 32], P('gx', 'gy', 'gz'), may hold values from 0 to 511, as said below
Outputs:
- coarse_matrix: bfloat16 [512, 64, 8192], P(('gx', 'gy', 'gz'))
The draws below stay inside these ranges and needn't reach their ends.
Inputs may be any that keep to these rules, and one draw needn't show every extreme that they name: `a_cols`: in each row the first a_count entries are distinct. `p_cols`: each row holds 0 to 7 once each, 0 in slot 0. `coarse_row`: values are distinct. Row r belongs to device r // 2 in mesh order; aggregate (u, v, w) goes to a row of a device with gx = u and gy = v. A device gets at most 2 aggregates, and in each group of devices with equal gx and gy one device gets exactly 2.
All inputs are finite; a program needn't handle non-finite values.
Results may differ from the reference program's by a relative error of at most 0.005.
Values may be sent and summed in bfloat16 or wider, within the bound.
No kernel may reach another device: no remote copies, remote signals or barrier semaphores. Data moves between devices by JAX's collectives and lax.ppermute only.
A program may use at most 192 MiB of HBM per device.

```python
import jax
import jax.numpy as jnp
from jax import lax

B = 64
K = 32
AZ = 1
NX = 4
NY = 8
NZ = 64
CAP = 2
ROWS = 512
N_GX = 2
N_GY = 4
N_GZ = 32


def draw_a_cols(key, part):
    row_count = NX * NY * NZ
    key_order, key_pad = jax.random.split(jax.random.fold_in(key, 11))
    scores = jax.random.randint(key_order, (row_count, 27), 0, 1 << 20) * 32 + jnp.arange(27)
    ordering = jnp.argsort(scores, axis=1).astype(jnp.int32)
    filler = jax.random.randint(key_pad, (row_count, K - 27), 0, 27).astype(jnp.int32)
    return jnp.concatenate([ordering, filler], axis=1).reshape(NX, NY, NZ, K).astype(jnp.int32)


def draw_p_cols(key, part):
    row_count = NX * NY * NZ
    scores = jax.random.randint(jax.random.fold_in(key, 13), (row_count, 7), 0, 1 << 20) * 8 + jnp.arange(7)
    ordering = jnp.argsort(scores, axis=1).astype(jnp.int32) + 1
    leading = jnp.zeros((row_count, 1), jnp.int32)
    return jnp.concatenate([leading, ordering], axis=1).reshape(NX, NY, NZ, 8).astype(jnp.int32)


def draw_coarse_row(key, part):
    group_count = N_GX * N_GY
    per_group = N_GZ * AZ

    def one_group(group_key, group_id):
        key_owner, key_order, key_other = jax.random.split(group_key, 3)
        busy_owner = jax.random.randint(key_owner, (), 0, N_GZ)
        ordering = jax.random.permutation(key_order, per_group)
        other_slots = jax.random.permutation(key_other, (N_GZ - 1) * CAP)[:per_group - CAP]
        other_slots = other_slots + CAP * (other_slots // CAP >= busy_owner).astype(jnp.int32)
        slot_list = jnp.concatenate([busy_owner * CAP + jnp.arange(CAP), other_slots]).astype(jnp.int32)
        chosen = jnp.zeros((per_group,), jnp.int32).at[ordering].set(slot_list)
        return group_id * N_GZ * CAP + chosen
    group_keys = jax.random.split(jax.random.fold_in(key, 29), group_count)
    result = jax.vmap(one_group)(group_keys, jnp.arange(group_count, dtype=jnp.int32))
    return result.reshape(N_GX, N_GY, per_group).astype(jnp.int32)


def plant(drawn, rng, low, largest):
    longest = drawn.shape.index(max(drawn.shape))
    spots = []
    for shift in (0, 1):
        where = [jax.random.randint(jax.random.fold_in(rng, axis), (), 0, length) for axis, length in enumerate(drawn.shape)]
        where[longest] = (where[longest] + shift) % drawn.shape[longest]
        spots.append(tuple(where))
    return drawn.at[spots[0]].set(low).at[spots[1]].set(largest)


def steps_of(rng, shape, cuts, least, high):
    def one(position, parts):
        steps = jax.random.uniform(jax.random.fold_in(jax.random.fold_in(rng, 6), position), (parts,), jnp.float32, least / len(cuts), high / len(cuts))
        return jnp.repeat(jnp.exp(steps), shape[position] // parts).reshape((-1,) + (1,) * (len(shape) - position - 1))

    gain = one(*cuts[0])
    for cut in cuts[1:]:
        gain = gain * one(*cut)
    return gain


def scatter_about(rng, shape, deviation, most, shards=(), kind=jnp.bfloat16):
    array = deviation * jax.random.normal(rng, shape, jnp.float32)
    if shards:
        array = array * steps_of(rng, shape, shards, -0.22, 0.18)
    return jnp.clip(array, -most, most).astype(kind)


def setup_inputs(seed: int = 0) -> dict:
    splits = jax.random.split(jax.random.key(seed), 8)
    a_blocks = scatter_about(splits[0], (NX, NY, NZ, B, K * B), (20 * B) ** -0.5, 0.15625, ((0, 2), (1, 4), (2, 32)))
    a_cols = draw_a_cols(jax.random.fold_in(splits[7], 71), 0)
    a_count = plant(jax.random.randint(splits[2], (NX, NY, NZ), 14, 28), jax.random.fold_in(splits[2], 1), 14, 27).astype(jnp.int32)
    p_blocks = scatter_about(splits[3], (NX, NY, NZ, B, 8 * B), B ** -0.5, 0.75, ((0, 2), (1, 4), (2, 32)))
    p_cols = draw_p_cols(jax.random.fold_in(splits[7], 71), 0)
    p_count = plant(jax.random.randint(splits[5], (NX, NY, NZ), 1, 9), jax.random.fold_in(splits[5], 1), 1, 8).astype(jnp.int32)
    coarse_row = draw_coarse_row(jax.random.fold_in(splits[7], 71), 0)
    return {"a_blocks": a_blocks, "a_cols": a_cols, "a_count": a_count, "p_blocks": p_blocks, "p_cols": p_cols, "p_count": p_count, "coarse_row": coarse_row}


CLASS_PICKS = ((0,), (1, 2), (3,))


def split_code(code_list):
    return code_list // 9 - 1, (code_list // 3) % 3 - 1, code_list % 3 - 1


def axis_slot(parity, offset, code_bit):
    landing = parity + offset
    shifted = jnp.floor_divide(landing, 2)
    facing = jnp.where(jnp.remainder(landing, 2) == 0, -1, 1)
    return shifted[:, None] + code_bit[None, :] * facing[:, None]


def slot_table(parity_x, parity_y, parity_z, code_list, live_count):
    offset_x, offset_y, offset_z = split_code(code_list)
    code_range = jnp.arange(8, dtype=jnp.int32)
    slot_x = axis_slot(parity_x, offset_x, code_range % 2)
    slot_y = axis_slot(parity_y, offset_y, (code_range // 2) % 2)
    slot_z = axis_slot(parity_z, offset_z, code_range // 4)
    target = (slot_x + 1) * 9 + (slot_y + 1) * 3 + (slot_z + 1)
    live = jnp.arange(code_list.shape[0], dtype=jnp.int32) < live_count
    return (target[:, :, None] == jnp.arange(28, dtype=jnp.int32)[None, None, :]) & live[:, None, None]


def place_rows(p_blocks, p_cols, p_count):
    shape_in = p_blocks.shape
    block_size = shape_in[3]
    blocks = p_blocks.astype(jnp.float32).reshape(shape_in[:3] + (block_size, 8, block_size))
    code_range = jnp.arange(8, dtype=jnp.int32)
    live = code_range < p_count[..., None]
    chooser = ((p_cols[..., None] == code_range) & live[..., None]).astype(jnp.float32)
    placed = jnp.einsum("xyzqc,xyzfqb->xyzfcb", chooser, blocks)
    return placed.astype(jnp.bfloat16).reshape(shape_in)


def coarse_sum(wide_placed, wide_product, block_size):
    extent = wide_product.shape[:3]
    groups = tuple((size_along - 2) // 2 for size_along in extent)
    total = jnp.zeros(groups + (block_size, 5, 5, 5, block_size), jnp.float32)
    for class_x in range(3):
        for class_y in range(3):
            for class_z in range(3):
                code = (class_x != 1) * 1 + (class_y != 1) * 2 + (class_z != 1) * 4
                partial_value = jnp.zeros(groups + (block_size, 28 * block_size), jnp.float32)
                for start_x in CLASS_PICKS[class_x]:
                    for start_y in CLASS_PICKS[class_y]:
                        for start_z in CLASS_PICKS[class_z]:
                            window = (slice(start_x, start_x + 2 * groups[0] - 1, 2),
                                      slice(start_y, start_y + 2 * groups[1] - 1, 2),
                                      slice(start_z, start_z + 2 * groups[2] - 1, 2))
                            blocks_p = wide_placed[window][..., code * block_size:(code + 1) * block_size].astype(jnp.float32)
                            blocks_ap = wide_product[window].astype(jnp.float32)
                            partial_value = partial_value + jnp.einsum("uvwfa,uvwfe->uvwae", blocks_p, blocks_ap)
                partial_value = partial_value.reshape(groups + (block_size, 28, block_size))[..., :27, :]
                partial_value = partial_value.reshape(groups + (block_size, 3, 3, 3, block_size))
                total = total.at[:, :, :, :, class_x:class_x + 3, class_y:class_y + 3, class_z:class_z + 3, :].add(partial_value)
    return total


def reference(a_blocks, a_cols, a_count, p_blocks, p_cols, p_count, coarse_row):
    placed = place_rows(p_blocks, p_cols, p_count)
    padded = jnp.pad(placed, ((1, 1), (1, 1), (1, 1), (0, 0), (0, 0)))
    flat_placed = padded.reshape(-1, B, 8 * B)
    total_rows = NX * NY * NZ
    row_ids = jnp.arange(total_rows, dtype=jnp.int32)
    coord_x = row_ids // (NY * NZ)
    coord_y = (row_ids // NZ) % NY
    coord_z = row_ids % NZ

    def one_row(row_item):
        row_blocks, code_list, live_count, at_x, at_y, at_z = row_item
        offset_x, offset_y, offset_z = split_code(code_list)
        flat_index = ((at_x + offset_x + 1) * (NY + 2) + (at_y + offset_y + 1)) * (NZ + 2) + (at_z + offset_z + 1)
        pieces = jnp.take(flat_placed, flat_index.astype(jnp.int32), axis=0).astype(jnp.float32).reshape(K, B, 8, B)
        chooser = slot_table(at_x % 2, at_y % 2, at_z % 2, code_list, live_count).astype(jnp.float32)
        a_row = row_blocks.astype(jnp.float32).reshape(B, K, B)
        partial_value = jnp.einsum("akc,kcqb->kaqb", a_row, pieces)
        summed = jnp.einsum("kqe,kaqb->aeb", chooser, partial_value, precision=lax.Precision.HIGHEST)
        return summed.reshape(B, 28 * B).astype(jnp.bfloat16)

    product = lax.map(one_row, (a_blocks.reshape(total_rows, B, K * B), a_cols.reshape(total_rows, K),
                                a_count.reshape(total_rows), coord_x, coord_y, coord_z))
    product = product.reshape(NX, NY, NZ, B, 28 * B)
    wide_product = jnp.pad(product, ((1, 1), (1, 1), (1, 1), (0, 0), (0, 0)))
    total = coarse_sum(padded, wide_product, B)
    coarse_rows = total.reshape(-1, B, 125 * B)
    coarse_rows = jnp.pad(coarse_rows, ((0, 0), (0, 0), (0, 3 * B))).astype(jnp.bfloat16)
    result = jnp.zeros((ROWS, B, 128 * B), jnp.bfloat16)
    return result.at[coarse_row.reshape(-1).astype(jnp.int32)].set(coarse_rows)
```

```python
import jax
import jax.numpy as jnp
from jax import lax
from jax.experimental import pallas as pl
from jax.experimental.pallas import tpu as pltpu
from jax.sharding import PartitionSpec as P

F32 = jnp.float32
BF16 = jnp.bfloat16
INTERPRET = False
VMEM = pl.BlockSpec(memory_space=pltpu.VMEM)
SMEM = pl.BlockSpec(memory_space=pltpu.SMEM)


def lanes_of(shape):
    return lax.broadcasted_iota(jnp.int32, shape, 1)


def half_turn(tile):
    return pltpu.roll(tile, 64, 1)


def doubled(pair, low):
    turned = half_turn(pair)
    return jnp.where(low, pair, turned), jnp.where(low, turned, pair)


def sort_kernel(spot_ref, p_ref, out_ref, sorted_ref):
    low = lanes_of((64, 128)) < 64
    half_of = lanes_of((64, 128)) // 64
    sorted_ref[...] = jnp.zeros(sorted_ref.shape, F32)
    for row in range(8):
        for slot_pair in range(4):
            pair = p_ref[row, :, 128 * slot_pair : 128 * slot_pair + 128].astype(F32)
            for side, block in enumerate(doubled(pair, low)):
                spot = spot_ref[row * 8 + slot_pair * 2 + side]
                at = row * 5 + spot // 2
                sorted_ref[at] = sorted_ref[at] + jnp.where(half_of == spot % 2, block, 0.0)
        for place in range(4):
            out_ref[row, :, 128 * place : 128 * place + 128] = sorted_ref[row * 5 + place].astype(
                BF16
            )


def product_kernel(spot_ref, a_ref, w_ref, own_ref, out_ref, left_ref, acc_ref, plain_ref, turn_ref, outer_ref, inner_ref):
    low = lanes_of((64, 128)) < 64
    half_of = lanes_of((64, 128)) // 64
    left_ref[...] = jnp.zeros(left_ref.shape, BF16)
    acc_ref[...] = jnp.zeros(acc_ref.shape, F32)
    outer_ref[...] = jnp.zeros(outer_ref.shape, BF16)
    inner_ref[...] = jnp.zeros(inner_ref.shape, BF16)

    def fill(row, carry):
        start = pl.multiple_of(row * 64, 64)
        for slot_pair in range(16):
            pair = a_ref[row, :, 128 * slot_pair : 128 * slot_pair + 128].astype(F32)
            for side, block in enumerate(doubled(pair, low)):
                spot = spot_ref[row * 32 + slot_pair * 2 + side]
                at = spot // 2
                piece = jnp.where(half_of == spot % 2, block, 0.0)
                old = left_ref[at, pl.ds(start, 64), :].astype(F32)
                left_ref[at, pl.ds(start, 64), :] = (old + piece).astype(BF16)
        return carry

    lax.fori_loop(0, 8, fill, 0)

    low_tall = lanes_of((512, 128)) < 64
    for hx in range(2):
        for hy in range(2):
            for hz in range(2):
                left = jnp.concatenate(
                    [
                        left_ref[((2 * hx + jx) * 4 + 2 * hy + jy) * 2 + hz]
                        for jx in range(2)
                        for jy in range(2)
                    ],
                    axis=1,
                )
                right = jnp.concatenate(
                    [
                        w_ref[((2 * hx + jx) * 4 + 2 * hy + jy) * 4 + 2 * hz + jz]
                        for jx in range(2)
                        for jy in range(2)
                        for jz in range(2)
                    ],
                    axis=0,
                )
                result = jnp.dot(left, right, preferred_element_type=F32)
                for bx in range(2):
                    for by in range(2):
                        at = (hx + bx) * 3 + hy + by
                        lane = (bx * 2 + by) * 128
                        piece = result[:, lane : lane + 128]
                        if hz == 0:
                            acc_ref[at, :, 0:128] += piece
                        else:
                            turned = half_turn(piece)
                            acc_ref[at, :, 0:128] += jnp.where(low_tall, 0.0, turned)
                            acc_ref[at, :, 128:256] += jnp.where(low_tall, turned, 0.0)
    for at in range(9):
        near = acc_ref[at, :, 0:128]
        far = acc_ref[at, :, 128:256]
        plain_ref[at, :, 0:128] = near.astype(BF16)
        plain_ref[at, :, 128:256] = far.astype(BF16)
        near_turned = half_turn(near)
        far_turned = half_turn(far)
        turn_ref[at, :, 0:128] = jnp.where(low_tall, 0.0, near_turned).astype(BF16)
        turn_ref[at, :, 128:256] = jnp.where(low_tall, near_turned, far_turned).astype(BF16)

    for vx in range(2):
        for vy in range(2):
            lane = (vx * 2 + vy) * 128
            for bx in range(2):
                for by in range(2):
                    group = (vx + bx) * 3 + vy + by
                    place = (bx * 2 + by) * 128
                    block = jnp.concatenate(
                        [
                            own_ref[(vx * 2 + vy) * 2 + vz, :, place : place + 128]
                            for vz in range(2)
                        ],
                        axis=0,
                    )
                    flipped = block.astype(F32).T
                    first, second = flipped[0:64], flipped[64:128]
                    outer_ref[group * 128 : group * 128 + 64, lane : lane + 128] = jnp.where(
                        low, first, 0.0
                    ).astype(BF16)
                    outer_ref[group * 128 + 64 : group * 128 + 128, lane : lane + 128] = jnp.where(
                        low, 0.0, second
                    ).astype(BF16)
                    inner_ref[group * 64 : group * 64 + 64, lane : lane + 128] = jnp.where(
                        low, second, first
                    ).astype(BF16)

    for at in range(9):
        lane = at * 256
        outer = jnp.dot(outer_ref[...], plain_ref[at], preferred_element_type=F32).astype(BF16)
        inner = jnp.dot(inner_ref[...], turn_ref[at], preferred_element_type=F32).astype(BF16)
        for group in range(9):
            out_ref[group, 0:128, lane : lane + 256] = outer[group * 128 : group * 128 + 128]
            out_ref[group, 128:192, lane : lane + 256] = inner[group * 64 : group * 64 + 64]


def finish_kernel(side_ref, own_ref, before_ref, after_ref, out_ref):
    low = lanes_of((64, 128)) < 64
    per_chunk = out_ref.shape[2] // 128

    def store(tile, value):
        lane = tile % per_chunk * 128
        out_ref[tile // per_chunk, :, lane : lane + 128] = value.astype(BF16)

    def column(ref, at, part):
        return ref[:, at * 256 + part * 128 : at * 256 + part * 128 + 128].astype(F32)

    tiles = []
    for pair in range(10):
        parts = []
        for at in (2 * pair, 2 * pair + 1):
            parts.append(
                (
                    column(own_ref, at, 0) + column(before_ref, at, 0),
                    column(own_ref, at, 1) + column(before_ref, at, 1) + column(after_ref, at, 0),
                    column(after_ref, at, 1),
                )
            )
        turned = [half_turn(tile) for tile in parts[1]]
        tiles += [
            parts[0][0],
            parts[0][1],
            jnp.where(low, parts[0][2], turned[0]),
            jnp.where(low, turned[0], turned[1]),
            jnp.where(low, turned[1], turned[2]),
        ]
    out_ref[...] = jnp.zeros(out_ref.shape, BF16)

    @pl.when(side_ref[0] == 1)
    def _():
        for at in range(50):
            store(at, tiles[at])

    @pl.when(side_ref[0] == 0)
    def _():
        last = jnp.zeros((64, 128), F32)
        for at in range(50):
            turned = half_turn(tiles[at])
            store(12 + at, jnp.where(low, last, turned))
            last = turned
        store(62, jnp.where(low, last, 0.0))


def pick_kernel(from_ref, live_ref, rows_ref, out_ref):
    def step(at, carry):
        @pl.when(live_ref[at] == 1)
        def _():
            out_ref[at] = rows_ref[from_ref[at]]

        @pl.when(live_ref[at] == 0)
        def _():
            out_ref[at] = jnp.zeros(out_ref.shape[1:], BF16)

        return carry

    lax.fori_loop(0, out_ref.shape[0], step, 0)


def call(kernel, out_shape, in_specs, scratch=()):
    return pl.pallas_call(
        kernel,
        out_shape=jax.ShapeDtypeStruct(out_shape, BF16),
        in_specs=in_specs,
        out_specs=VMEM,
        scratch_shapes=list(scratch),
        compiler_params=pltpu.CompilerParams(vmem_limit_bytes=58 * 1024 * 1024),
        interpret=INTERPRET,
    )


def chain(axis):
    size = lax.axis_size(axis)
    return [(i, i + 1) for i in range(size - 1)], [(i + 1, i) for i in range(size - 1)]


def local(a_blocks, a_cols, a_count, p_blocks, p_cols, p_count, coarse_row):
    side = lax.axis_index("gx")
    lower = side == 0
    group_size = lax.axis_size("gz")
    swap = [(0, 1), (1, 0)]
    up_y, down_y = chain("gy")
    up_z, down_z = chain("gz")

    group_base = (side * lax.axis_size("gy") + lax.axis_index("gy")) * group_size * 2
    targets = lax.all_gather(coarse_row.reshape(1), "gz", tiled=True) - group_base
    hits = jnp.arange(2 * group_size, dtype=jnp.int32)[:, None] == targets[None, :]
    source = jnp.sum(
        jnp.where(hits, jnp.arange(group_size, dtype=jnp.int32)[None, :], 0), axis=1
    ).astype(jnp.int32)
    live = jnp.any(hits, axis=1).astype(jnp.int32)

    row_ids = jnp.arange(8, dtype=jnp.int32)[:, None]
    row_x, row_y, row_z = row_ids // 4, row_ids // 2 % 2, row_ids % 2

    codes = p_cols.reshape(8, 8)
    place_x = codes % 2 ^ (1 - row_x)
    place_y = codes // 2 % 2 ^ (1 - row_y)
    place_z = codes // 4 ^ (1 - row_z)
    p_spot = jnp.where(
        jnp.arange(8, dtype=jnp.int32)[None, :] < p_count.reshape(8, 1),
        place_x * 4 + place_y * 2 + place_z,
        8,
    )
    placed = call(sort_kernel, (8, 64, 512), [SMEM, VMEM], [pltpu.VMEM((40, 64, 128), F32)])(
        p_spot.reshape(-1), p_blocks.reshape(8, 64, 512)
    )

    wide = placed.reshape(2, 2, 2, 64, 512)
    wide = jnp.concatenate(
        [
            lax.ppermute(wide[:, :, 1:2], "gz", up_z),
            wide,
            lax.ppermute(wide[:, :, 0:1], "gz", down_z),
        ],
        axis=2,
    )
    wide = jnp.concatenate(
        [
            lax.ppermute(wide[:, 1:2], "gy", up_y),
            wide,
            lax.ppermute(wide[:, 0:1], "gy", down_y),
        ],
        axis=1,
    )
    facing = lax.ppermute(jnp.where(lower, wide[1:2], wide[0:1]), "gx", swap)
    nothing = jnp.zeros((), BF16)
    wide = jnp.concatenate(
        [jnp.where(lower, nothing, facing), wide, jnp.where(lower, facing, nothing)], axis=0
    )

    neighbours = a_cols.reshape(8, 32)
    at_x = row_x + neighbours // 9
    at_y = row_y + neighbours // 3 % 3
    at_z = row_z + neighbours % 3
    a_spot = jnp.where(
        jnp.arange(32, dtype=jnp.int32)[None, :] < a_count.reshape(8, 1),
        (at_x * 4 + at_y) * 4 + at_z,
        64,
    )
    parts = call(
        product_kernel,
        (9, 192, 2304),
        [SMEM, VMEM, VMEM, VMEM],
        [
            pltpu.VMEM((33, 512, 128), BF16),
            pltpu.VMEM((9, 512, 256), F32),
            pltpu.VMEM((9, 512, 256), BF16),
            pltpu.VMEM((9, 512, 256), BF16),
            pltpu.VMEM((1152, 512), BF16),
            pltpu.VMEM((576, 512), BF16),
        ],
    )(
        a_spot.reshape(-1),
        a_blocks.reshape(8, 64, 2048),
        wide.reshape(64, 64, 512),
        placed,
    )
    parts = parts.reshape(3, 3, 192, 2304)

    own = parts[1]
    came = lax.ppermute(jnp.where(lower, parts[2], parts[0]), "gx", swap)
    first = jnp.where(lower, own, came).astype(F32)
    second = jnp.where(lower, came, own).astype(F32)
    summed = jnp.pad(first, ((0, 0), (0, 0), (0, 768))) + jnp.pad(
        second, ((0, 0), (0, 0), (768, 0))
    )
    summed = summed.astype(BF16)

    before = lax.ppermute(summed[2], "gy", up_y)
    after = lax.ppermute(summed[0], "gy", down_y)

    def widened(field, shift):
        field = field.reshape(192, 4, 768).astype(F32)
        return jnp.pad(field, ((0, 0), (0, 0), (256 * shift, 512 - 256 * shift)))

    summed = widened(before, 0) + widened(summed[1], 1) + widened(after, 2)
    summed = summed.astype(BF16).reshape(192, 5120)

    before = lax.ppermute(summed[64:128], "gz", up_z)
    after = lax.ppermute(summed[0:64], "gz", down_z)
    width = 8192 // group_size
    chunks = call(finish_kernel, (group_size, 64, width), [SMEM, VMEM, VMEM, VMEM])(
        side.astype(jnp.int32).reshape(1), summed[128:192], before, after
    )

    rows = lax.all_to_all(chunks, "gz", split_axis=0, concat_axis=0, tiled=True)
    picked = call(pick_kernel, (2 * group_size, 64, width), [SMEM, SMEM, VMEM])(source, live, rows)
    landed = lax.all_to_all(picked, "gz", split_axis=0, concat_axis=0, tiled=True)
    landed = landed.reshape(group_size, 2, 64, width)
    return jnp.transpose(landed, (1, 2, 0, 3)).reshape(2, 64, 8192)


def solution(mesh):
    in_specs = (
        P("gx", "gy", "gz", None, None),
        P("gx", "gy", "gz", None),
        P("gx", "gy", "gz"),
        P("gx", "gy", "gz", None, None),
        P("gx", "gy", "gz", None),
        P("gx", "gy", "gz"),
        P("gx", "gy", "gz"),
    )
    out_specs = P(("gx", "gy", "gz"), None, None)
    return jax.shard_map(local, mesh=mesh, in_specs=in_specs, out_specs=out_specs, check_vma=False)
```
